256 devices in a mesh: space: 128 (over z, x, y), sub: 2 (over core).
Axes of the slice: x: 4, y: 4, z: 8, core: 2. Of those that a mesh axis runs over, the one named last changes fastest.
Arguments:
- fields: bfloat16 [1048576, 256], P(('space', 'sub')), may hold values from -6 to 6
- kriging: bfloat16 [4096, 256, 768], P(('space', 'sub')), may hold values from -0.21875 to 0.21875
- whitening: bfloat16 [4096, 256, 256], P(('space', 'sub')), may hold values from -0.375 to 0.375
- neighbours: int32 [4096, 3], P(('space', 'sub')), may hold values from 0 to 4095, as said below
- home: int32 [4096], replicated, may hold values from 0 to 4095, as said below
Outputs:
- gradient: bfloat16 [1048576, 256], P(('space', 'sub'))
The draws below stay inside these ranges and needn't reach their ends.
Inputs may be any that keep to these rules, and one draw needn't show every extreme that they name: `home`: A permutation of the slots that maps the block ids of every region onto that region's own slots. `neighbours`: the 3 x 16 references of one device name different blocks, none stored on that device. Each lies in the device's own region or in the region 1 or 2 before it along space, counting cyclically. At most 20 references of one device name blocks of one earlier region, and every device has exactly 20 towards one of its two earlier regions.
All inputs are finite; a program needn't handle non-finite values.
Results may differ from the reference program's by a relative error of at most 0.006.
Values may be sent and summed in bfloat16 or wider, within the bound.
No kernel may reach another device: no remote copies, remote signals or barrier semaphores. Data moves between devices by JAX's collectives and lax.ppermute only.
A program may use at most 128 MiB of HBM per device.

```python
import jax
import jax.numpy as jnp
from jax import lax

PTS = 256
NBR = 3
BLK_DEV = 16
FIELDS = 256
REACH = 2
CAP = 20
ORDER = 768
REGION = 32
REGIONS = 128
NBLK = 4096


def region_maps(key):
    perm_keys = jax.random.split(jax.random.fold_in(key, 11), REGIONS)
    orders = jax.vmap(lambda sub_key: jax.random.permutation(sub_key, REGION))(perm_keys).astype(jnp.int32)
    bases = (jnp.arange(REGIONS, dtype=jnp.int32) * REGION)[:, None]
    home_map = (bases + orders).reshape(-1).astype(jnp.int32)
    inverse = (bases + jnp.argsort(orders, axis=1).astype(jnp.int32)).reshape(-1).astype(jnp.int32)
    return (home_map, inverse)


def draw_home(key, part):
    return region_maps(key)[0]


def draw_neighbours(key, part):
    home_map, inverse = region_maps(key)
    device_total = NBLK // BLK_DEV
    core_total = REGION // BLK_DEV
    reference_total = NBR * BLK_DEV
    device_keys = jax.random.split(jax.random.fold_in(key, 23), device_total)

    def one_device(sub_key, device):
        region_index = device // core_total
        core_index = device % core_total
        key_list = jax.random.split(sub_key, 6)
        local_count = jax.random.randint(key_list[0], (), 3 * BLK_DEV // 4, BLK_DEV + 1)
        full_step = jax.random.randint(key_list[1], (), 1, REACH + 1)
        placed = jax.random.permutation(key_list[2], reference_total).astype(jnp.int32)
        order_near = jax.random.permutation(key_list[3], REGION - BLK_DEV).astype(jnp.int32)
        order_full = jax.random.permutation(key_list[4], REGION).astype(jnp.int32)
        order_other = jax.random.permutation(key_list[5], REGION).astype(jnp.int32)
        position = jnp.arange(reference_total, dtype=jnp.int32)
        other_start = local_count + CAP
        category_step = jnp.where(position < local_count, 0, jnp.where(position < other_start, full_step, REACH + 1 - full_step))
        index_within = jnp.where(position < local_count, position, jnp.where(position < other_start, position - local_count, position - other_start))
        near_pick = order_near[jnp.clip(index_within, 0, REGION - BLK_DEV - 1)]
        near_local = jnp.where(near_pick >= core_index * BLK_DEV, near_pick + BLK_DEV, near_pick)
        far_index = jnp.clip(index_within, 0, REGION - 1)
        far_pick = jnp.where(position < other_start, order_full[far_index], order_other[far_index])
        local_slot = jnp.where(category_step == 0, near_local, far_pick)
        region_of = (region_index - category_step) % REGIONS
        slot_value = region_of * REGION + local_slot
        block_ids = inverse[slot_value]
        return block_ids[jnp.argsort(placed)].astype(jnp.int32)
    table = jax.vmap(one_device)(device_keys, jnp.arange(device_total, dtype=jnp.int32))
    return table.reshape(NBLK, NBR).astype(jnp.int32)


def level_of(rng, dims, shards, smallest, top_value):
    def one(dim, blocks):
        draws = jax.random.uniform(jax.random.fold_in(jax.random.fold_in(rng, 6), dim), (blocks,), jnp.float32, smallest / len(shards), top_value / len(shards))
        return jnp.repeat(jnp.exp(draws), dims[dim] // blocks).reshape((-1,) + (1,) * (len(dims) - dim - 1))

    loudness = one(*shards[0])
    for cut in shards[1:]:
        loudness = loudness * one(*cut)
    return loudness


def scatter_about(own_key, dims, width, limit, cuts=(), kind=jnp.bfloat16):
    factor_of = level_of(own_key, dims, cuts, -0.22, 0.18) if cuts else 1.0
    array = jax.random.normal(own_key, dims, jnp.float32) * width * factor_of
    return jnp.minimum(jnp.maximum(array, -limit), limit).astype(kind)


def setup_inputs(seed: int = 0) -> dict:
    keys = jax.random.split(jax.random.key(seed), 6)
    return {
        "fields": scatter_about(keys[0], (NBLK * PTS, FIELDS), 1.0, 6.0, ((0, 256),)),
        "kriging": scatter_about(keys[1], (NBLK, PTS, ORDER), ORDER ** -0.5, 0.21875, ((0, 256),)),
        "whitening": scatter_about(keys[2], (NBLK, PTS, PTS), PTS ** -0.5, 0.375, ((0, 256),)),
        "neighbours": draw_neighbours(jax.random.fold_in(keys[5], 71), 0),
        "home": draw_home(jax.random.fold_in(keys[5], 71), 0),
    }


def reference(fields, kriging, whitening, neighbours, home):
    block_total = neighbours.shape[0]
    series = fields.shape[1]
    blocks = fields.reshape(block_total, PTS, series)
    slot_table = jnp.take(home, neighbours.reshape(-1)).reshape(block_total, NBR).astype(jnp.int32)
    group_count = block_total // BLK_DEV

    def one_group(accumulated, group):
        first_block = (group * BLK_DEV).astype(jnp.int32)
        own_fields = lax.dynamic_slice_in_dim(blocks, first_block, BLK_DEV, 0).astype(jnp.float32)
        kriging_part = lax.dynamic_slice_in_dim(kriging, first_block, BLK_DEV, 0).astype(jnp.float32)
        whitening_part = lax.dynamic_slice_in_dim(whitening, first_block, BLK_DEV, 0).astype(jnp.float32)
        slot_part = lax.dynamic_slice_in_dim(slot_table, first_block, BLK_DEV, 0).reshape(-1).astype(jnp.int32)
        neighbourhood = jnp.take(blocks, slot_part, axis=0).reshape(BLK_DEV, ORDER, series).astype(jnp.float32)
        prediction = jnp.einsum("bpk,bks->bps", kriging_part, neighbourhood)
        residual = lax.optimization_barrier((own_fields - prediction).astype(jnp.bfloat16)).astype(jnp.float32)
        whitened = jnp.einsum("bpq,bqs->bps", whitening_part, residual)
        whitened = lax.optimization_barrier(whitened.astype(jnp.bfloat16)).astype(jnp.float32)
        pulled = jnp.einsum("bqp,bqs->bps", whitening_part, whitened)
        pulled = lax.optimization_barrier(pulled.astype(jnp.bfloat16)).astype(jnp.float32)
        returned = jnp.einsum("bpk,bps->bks", kriging_part, pulled)
        returned = lax.optimization_barrier(returned.astype(jnp.bfloat16)).astype(jnp.float32)
        accumulated = accumulated.at[slot_part].add(returned.reshape(BLK_DEV * NBR, PTS, series))
        current = lax.dynamic_slice_in_dim(accumulated, first_block, BLK_DEV, 0)
        accumulated = lax.dynamic_update_slice_in_dim(accumulated, current - pulled, first_block, 0)
        return accumulated, None

    start_value = jnp.zeros((block_total, PTS, series), jnp.float32)
    result, unused = lax.scan(one_group, start_value, jnp.arange(group_count, dtype=jnp.int32))
    return result.reshape(block_total * PTS, series).astype(jnp.bfloat16)
```

```python
import functools

import jax
import jax.numpy as jnp
from jax import lax
from jax.experimental import pallas as pl
from jax.experimental.pallas import tpu as pltpu
from jax.sharding import PartitionSpec as P

X, Y, Z = 4, 4, 8
SWAP = ((0, 1), (1, 0))

AHEAD = ((0, 5), (5, 10))
BEHIND = ((10, 13), (13, 16))


def region_of(z, x, y):
    return (z % Z) * X * Y + (x % X) * Y + y % Y


def chip_of(region):
    return region // (X * Y), region // Y % X, region % Y


def hops():
    count = X * Y * Z
    every = range(count)
    forward = [(r, (r + 1) % count) for r in every]
    first, second = [], []
    for r in every:
        z, x, y = chip_of(r)
        relay = region_of(z, x, y - 1)
        first.append((r, relay))
        second.append((relay, (r + 2) % count))
    third = [(r, (r - 1) % count) for r in every]
    return forward, first, second, third


def reverse(pairs):
    return [(target, source) for source, target in pairs]


def compute(block_count, pieces, place, own, kriging, whitening, *refs):
    piece_count = len(pieces)
    tables = refs[:piece_count]
    shares = refs[piece_count : 2 * piece_count]
    pulled_out = refs[2 * piece_count]
    table, share, own_v, krig_v, white_v, pulled_v, t_sem, b_sem, o_sem = refs[2 * piece_count + 1 :]
    points = own.shape[1]
    table_copies = [
        pltpu.make_async_copy(tables[i], table.at[pl.ds(start, size)], t_sem.at[i])
        for i, (start, size) in enumerate(pieces)
    ]
    for copy in table_copies:
        copy.start()

    def block_copies(b):
        return (
            pltpu.make_async_copy(kriging.at[b], krig_v.at[b], b_sem.at[0, b]),
            pltpu.make_async_copy(own.at[b], own_v.at[b], b_sem.at[1, b]),
            pltpu.make_async_copy(whitening.at[b], white_v.at[b], b_sem.at[2, b]),
        )

    @pl.loop(0, block_count)
    def _(b):
        for copy in block_copies(b):
            copy.start()

    @pl.loop(0, share.shape[0])
    def _(i):
        share[i] = jnp.zeros(share.shape[1:], share.dtype)

    for copy in table_copies:
        copy.wait()

    neighbours = krig_v.shape[2] // points

    @pl.loop(0, block_count)
    def _(b):
        for copy in block_copies(b):
            copy.wait()
        total = None
        for k in range(neighbours):
            term = jnp.dot(
                krig_v[b, :, k * points : (k + 1) * points],
                table[place[b * neighbours + k]],
                preferred_element_type=jnp.float32,
            )
            total = term if total is None else total + term
        residual = (own_v[b].astype(jnp.float32) - total).astype(jnp.bfloat16)
        factor = white_v[b]
        whitened = jnp.dot(factor, residual, preferred_element_type=jnp.float32).astype(jnp.bfloat16)
        pulled = lax.dot_general(
            factor, whitened, (((0,), (0,)), ((), ())), preferred_element_type=jnp.float32
        ).astype(jnp.bfloat16)
        pulled_v[b] = pulled
        for k in range(neighbours):
            returned = lax.dot_general(
                krig_v[b, :, k * points : (k + 1) * points],
                pulled,
                (((0,), (0,)), ((), ())),
                preferred_element_type=jnp.float32,
            )
            share[place[b * neighbours + k]] = returned.astype(jnp.bfloat16)

    out_copies = [
        pltpu.make_async_copy(share.at[pl.ds(start, size)], shares[i], o_sem.at[i])
        for i, (start, size) in enumerate(pieces)
    ]
    out_copies.append(pltpu.make_async_copy(pulled_v, pulled_out, o_sem.at[piece_count]))
    for copy in out_copies:
        copy.start()
    for copy in out_copies:
        copy.wait()


def add(a, b):
    return (a.astype(jnp.float32) + b.astype(jnp.float32)).astype(jnp.bfloat16)


def body(fields, kriging, whitening, neighbours, home):
    block_count, points, order_size = kriging.shape
    series = fields.shape[1]
    core_count = lax.axis_size("sub")
    region_count = lax.axis_size("space")
    region_size = block_count * core_count
    region_index = lax.axis_index("space")
    core_index = lax.axis_index("sub")
    forward, first, second, third = hops()

    def swap(value):
        return lax.ppermute(value, "sub", SWAP)

    def send(value, pairs):
        return lax.ppermute(value, "space", pairs)

    slot_ids = jnp.take(home, neighbours.reshape(-1))
    distance = (region_index - slot_ids // region_size) % region_count
    within = slot_ids % region_size
    other = jnp.where(within // block_count == core_index, 0, block_count)
    place = distance * region_size + other + within % block_count - block_count
    place = place.astype(jnp.int32)

    own = fields.reshape(block_count, points, series)
    pieces = [(0, block_count)]
    arrays = [swap(own)]
    near, far = block_count, block_count + region_size
    for start, stop in AHEAD:
        one = send(own[start:stop], forward)
        two = send(one, forward)
        size = stop - start
        pieces += [(near + start, size), (near + block_count + start, size)]
        pieces += [(far + start, size), (far + block_count + start, size)]
        arrays += [one, swap(one), two, swap(two)]
    for start, stop in BEHIND:
        two = send(send(own[start:stop], first), second)
        one = send(two, third)
        size = stop - start
        pieces += [(near + start, size), (near + block_count + start, size)]
        pieces += [(far + start, size), (far + block_count + start, size)]
        arrays += [one, swap(one), two, swap(two)]

    table_size = block_count + 2 * region_size
    any_spec = pl.BlockSpec(memory_space=pl.ANY)
    block_shape = (points, series)
    out_shape = [jax.ShapeDtypeStruct((size, *block_shape), jnp.bfloat16) for _, size in pieces]
    out_shape.append(jax.ShapeDtypeStruct((block_count, *block_shape), jnp.bfloat16))
    flops = 2 * block_count * points * points * series * 8
    outs = pl.pallas_call(
        functools.partial(compute, block_count, pieces),
        out_shape=out_shape,
        in_specs=[pl.BlockSpec(memory_space=pltpu.SMEM)] + [any_spec] * (3 + len(pieces)),
        out_specs=[any_spec] * len(out_shape),
        scratch_shapes=[
            pltpu.VMEM((table_size, *block_shape), jnp.bfloat16),
            pltpu.VMEM((table_size, *block_shape), jnp.bfloat16),
            pltpu.VMEM((block_count, *block_shape), jnp.bfloat16),
            pltpu.VMEM((block_count, points, order_size), jnp.bfloat16),
            pltpu.VMEM((block_count, points, points), jnp.bfloat16),
            pltpu.VMEM((block_count, *block_shape), jnp.bfloat16),
            pltpu.SemaphoreType.DMA((len(pieces),)),
            pltpu.SemaphoreType.DMA((3, block_count)),
            pltpu.SemaphoreType.DMA((len(pieces) + 1,)),
        ],
        cost_estimate=pl.CostEstimate(flops=flops, bytes_accessed=34 << 20, transcendentals=0),
        compiler_params=pltpu.CompilerParams(vmem_limit_bytes=56 << 20),
        name="blocks",
    )(place, own, kriging, whitening, *arrays)
    pulled = outs[-1]
    home_share = swap(outs[0])
    gradient = []
    index = 1
    for _ in AHEAD:
        near_own, near_other, far_own, far_other = outs[index : index + 4]
        index += 4
        two = add(far_own, swap(far_other))
        one = add(near_own, swap(near_other))
        gradient.append(send(add(send(two, reverse(forward)), one), reverse(forward)))
    for _ in BEHIND:
        near_own, near_other, far_own, far_other = outs[index : index + 4]
        index += 4
        one = add(near_own, swap(near_other))
        two = add(far_own, swap(far_other))
        total = add(send(one, reverse(third)), two)
        gradient.append(send(send(total, reverse(second)), reverse(first)))
    parts = []
    for (start, stop), arrived in zip(AHEAD + BEHIND, gradient):
        parts.append(
            arrived.astype(jnp.float32)
            + home_share[start:stop].astype(jnp.float32)
            - pulled[start:stop].astype(jnp.float32)
        )
    return jnp.concatenate(parts, axis=0).astype(jnp.bfloat16).reshape(fields.shape)


def solution(mesh):
    return jax.shard_map(
        body,
        mesh=mesh,
        in_specs=(
            P(("space", "sub"), None),
            P(("space", "sub"), None, None),
            P(("space", "sub"), None, None),
            P(("space", "sub"), None),
            P(),
        ),
        out_specs=P(("space", "sub"), None),
        check_vma=False,
    )
```
